256 devices in a mesh: row: 16 (over y, x), col: 16 (over z, core).
Axes of the slice: x: 4, y: 4, z: 8, core: 2. Of those that a mesh axis runs over, the one named last changes fastest.
Arguments:
- trailing_slab: bfloat16 [98304, 8192], P('row', 'col'), may hold values from -6 to 6
- panel_cols: bfloat16 [98304, 512], P('row', 'col'), may hold values from -0.25 to 0.25
- head_slab: bfloat16 [512, 8192], P('row', 'col'), may hold values from -6 to 6
- coupling: bfloat16 [2, 256, 256], replicated, may hold values from -0.25 to 0.25
- lower_inverses: bfloat16 [2, 256, 256], replicated, may hold values from -1.5 to 1.5, as said below
- upper_inverses: bfloat16 [2, 256, 256], replicated, may hold values from -1.5 to 1.5, as said below
Outputs:
- trailing: bfloat16 [98304, 8192], P('row', 'col')
The draws below stay inside these ranges and needn't reach their ends.
Inputs may be any that keep to these rules, and one draw needn't show every extreme that they name: `lower_inverses`: each of the two [256, 256] blocks is lower triangular with unit diagonal. `upper_inverses`: each of the two [256, 256] blocks is upper triangular with diagonal between 0.5 and 1.5.
All inputs are finite; a program needn't handle non-finite values.
Results may differ from the reference program's by a relative error of at most 0.0067.
Values may be sent and summed in bfloat16 or wider, within the bound.
A program may use at most 128 MiB of HBM per device.

```python
import math
import jax
import jax.numpy as jnp
from jax import lax

NB = 256
TRAIL = 8192
ROWS_DEV = 6144
MROWS = 98304


def off_diagonal(key):
    values = jax.random.normal(key, (2, NB, NB), jnp.float32)
    return jnp.clip(values, -4.0, 4.0) * (0.5 / math.sqrt(NB))


def draw_lower_inverses(key, part):
    values = off_diagonal(jax.random.fold_in(key, 11))
    row_ids = lax.broadcasted_iota(jnp.int32, (2, NB, NB), 1)
    col_ids = lax.broadcasted_iota(jnp.int32, (2, NB, NB), 2)
    return (jnp.where(row_ids > col_ids, values, 0.0) + jnp.where(row_ids == col_ids, 1.0, 0.0)).astype(jnp.bfloat16)


def draw_upper_inverses(key, part):
    values = off_diagonal(jax.random.fold_in(key, 23))
    diag_values = jax.random.uniform(jax.random.fold_in(key, 37), (2, NB, NB), jnp.float32, 0.5, 1.5)
    row_ids = lax.broadcasted_iota(jnp.int32, (2, NB, NB), 1)
    col_ids = lax.broadcasted_iota(jnp.int32, (2, NB, NB), 2)
    return (jnp.where(row_ids < col_ids, values, 0.0) + jnp.where(row_ids == col_ids, diag_values, 0.0)).astype(jnp.bfloat16)


def block_scale(stream_key, shape, shards, least, top_value):
    factor_of = 1.0
    for axis_at, blocks in shards:
        heights = jax.random.uniform(jax.random.fold_in(jax.random.fold_in(stream_key, 6), axis_at), (blocks,), jnp.float32, least / len(shards), top_value / len(shards))
        factor_of = factor_of * jnp.repeat(jnp.exp(heights), shape[axis_at] // blocks).reshape((-1,) + (1,) * (len(shape) - 1 - axis_at))
    return factor_of


def scatter_about(stream_key, extent, scale, bound, pieces=(), dtype=jnp.bfloat16):
    level = block_scale(stream_key, extent, pieces, -0.22, 0.18) if pieces else 1.0
    drawn = jax.random.normal(stream_key, extent, jnp.float32) * scale * level
    return jnp.minimum(jnp.maximum(drawn, -bound), bound).astype(dtype)


def setup_inputs(seed: int = 0) -> dict:
    key_of = jax.random.split(jax.random.key(seed), 7)
    trailing_slab = scatter_about(key_of[0], (MROWS, TRAIL), 1.0, 6.0, ((0, 16), (1, 16)))
    panel_cols = scatter_about(key_of[1], (MROWS, 2 * NB), (2 * NB) ** -0.5, 0.25, ((0, 16), (1, 16)))
    head_slab = scatter_about(key_of[2], (2 * NB, TRAIL), 1.0, 6.0, ((0, 16), (1, 16)))
    coupling = scatter_about(key_of[3], (2, NB, NB), (2 * NB) ** -0.5, 0.25)
    lower_inverses = draw_lower_inverses(jax.random.fold_in(key_of[6], 71), 0)
    upper_inverses = draw_upper_inverses(jax.random.fold_in(key_of[6], 71), 0)
    return {"trailing_slab": trailing_slab, "panel_cols": panel_cols, "head_slab": head_slab, "coupling": coupling, "lower_inverses": lower_inverses, "upper_inverses": upper_inverses}


def product(left, right):
    return jnp.dot(left, right, preferred_element_type=jnp.float32)


def reference(trailing_slab, panel_cols, head_slab, coupling, lower_inverses, upper_inverses):
    lower_first = product(panel_cols[:, :NB], upper_inverses[0]).astype(jnp.bfloat16)
    upper_mid = product(lower_inverses[0], coupling[0]).astype(jnp.bfloat16)
    upper_first = product(lower_inverses[0], head_slab[:NB]).astype(jnp.bfloat16)
    lower_head = product(coupling[1], upper_inverses[0]).astype(jnp.bfloat16)
    panel_second = (panel_cols[:, NB:].astype(jnp.float32) - product(lower_first, upper_mid)).astype(jnp.bfloat16)
    lower_second = product(panel_second, upper_inverses[1]).astype(jnp.bfloat16)
    head_second = (head_slab[NB:].astype(jnp.float32) - product(lower_head, upper_first)).astype(jnp.bfloat16)
    upper_second = product(lower_inverses[1], head_second).astype(jnp.bfloat16)
    blocks = MROWS // ROWS_DEV
    slab_blocks = trailing_slab.reshape(blocks, ROWS_DEV, TRAIL)
    first_blocks = lower_first.reshape(blocks, ROWS_DEV, NB)
    second_blocks = lower_second.reshape(blocks, ROWS_DEV, NB)

    def update(items):
        slab_part, first_part, second_part = items
        result = slab_part.astype(jnp.float32) - product(first_part, upper_first) - product(second_part, upper_second)
        return result.astype(jnp.bfloat16)

    updated = lax.map(update, (slab_blocks, first_blocks, second_blocks))
    return updated.reshape(MROWS, TRAIL)
```

```python
import functools

import jax
import jax.numpy as jnp
from jax import lax
from jax.experimental import pallas as pl
from jax.experimental.pallas import tpu as pltpu
from jax.sharding import PartitionSpec as P

MESH = pl.DeviceIdType.MESH
BF16 = jnp.bfloat16
F32 = jnp.float32
BATCH = 8
CHUNKS = 2 * BATCH
DEPTH = 8


def product(left, right):
    return jnp.dot(left, right, preferred_element_type=F32)


def update_kernel(
    slab_hbm, panel_hbm, head_hbm, coupling_hbm, lower_hbm, upper_hbm,
    out,
    gathered, head_full, coupling, lower_inv, upper_inv, mid, factors,
    local_sem, ring_send, pair_send, head_send, ring_recv, pair_recv, head_recv,
):
    chunks, width2, rows = gathered.shape
    width = width2 // 2
    share = panel_hbm.shape[0]
    head_share = head_hbm.shape[0]
    row = lax.axis_index("row")
    col = lax.axis_index("col")
    n_row = lax.axis_size("row")
    depth = lax.axis_size("col") // 2
    z, core = col // 2, col % 2
    ahead = ((z + 1) % depth) * 2 + core
    behind = ((z + depth - 1) % depth) * 2 + core
    other = z * 2 + (1 - core)

    barrier = pltpu.get_barrier_semaphore()
    for peer in (ahead, behind, other):
        pl.semaphore_signal(barrier, inc=1, device_id=(row, peer), device_id_type=MESH)
    for step in range(1, n_row):
        pl.semaphore_signal(
            barrier, inc=1, device_id=((row + step) % n_row, col), device_id_type=MESH
        )

    def block_rows(hops):
        source = ((z + depth - hops) % depth) * 2 + core
        return pl.ds(pl.multiple_of(source * share, share), share)

    own_rows = block_rows(0)
    head_rows = pl.ds(pl.multiple_of(row * head_share, head_share), head_share)

    for chunk in range(chunks):
        pltpu.make_async_copy(
            panel_hbm.at[:, pl.ds(chunk * rows, rows)],
            gathered.at[chunk, own_rows],
            local_sem.at[0],
        ).start()
    head_copy = pltpu.make_async_copy(head_hbm, head_full.at[head_rows], local_sem.at[1])
    head_copy.start()
    small_copies = [
        pltpu.make_async_copy(source, target, local_sem.at[at])
        for source, target, at in (
            (coupling_hbm, coupling, 2), (lower_hbm, lower_inv, 3), (upper_hbm, upper_inv, 4),
            (slab_hbm, out, 5),
        )
    ]
    for copy in small_copies:
        copy.start()
    pltpu.make_async_copy(
        gathered.at[:, own_rows], gathered.at[:, own_rows], local_sem.at[0]
    ).wait()
    head_copy.wait()
    pl.semaphore_wait(barrier, 3 + n_row - 1)

    def ring_copy(direction, hop, chunk):
        hops = hop - 1 if direction == 0 else depth - (hop - 1)
        where = block_rows(hops)
        return pltpu.make_async_remote_copy(
            src_ref=gathered.at[chunk, where],
            dst_ref=gathered.at[chunk, where],
            send_sem=ring_send,
            recv_sem=ring_recv.at[direction, hop - 1, chunk],
            device_id=(row, ahead if direction == 0 else behind),
            device_id_type=MESH,
        )

    def ring_arrived(direction, hop, chunk):
        hops = hop if direction == 0 else depth - hop
        where = block_rows(hops)
        pltpu.make_async_remote_copy(
            src_ref=gathered.at[chunk, where],
            dst_ref=gathered.at[chunk, where],
            send_sem=ring_send,
            recv_sem=ring_recv.at[direction, hop - 1, chunk],
            device_id=(row, ahead if direction == 0 else behind),
            device_id_type=MESH,
        ).wait_recv()

    def pair_copy(direction, hop, chunk):
        hops = hop if direction == 0 else depth - hop
        where = block_rows(hops)
        return pltpu.make_async_remote_copy(
            src_ref=gathered.at[chunk, where],
            dst_ref=gathered.at[chunk, where],
            send_sem=pair_send,
            recv_sem=pair_recv.at[chunk],
            device_id=(row, other),
            device_id_type=MESH,
        )

    def send_own(chunk):
        ring_copy(0, 1, chunk).start()
        ring_copy(1, 1, chunk).start()
        pair_copy(0, 0, chunk).start()

    def forward(direction, hop, chunk):
        ring_arrived(direction, hop, chunk)
        ring_copy(direction, hop + 1, chunk).start()
        pair_copy(direction, hop, chunk).start()

    def keep(direction, hop, chunk):
        ring_arrived(direction, hop, chunk)
        pair_copy(direction, hop, chunk).start()

    half = BATCH // 2

    def compute(chunk):
        every = pl.ds(0, width2)
        other_half = gathered.at[chunk, pl.ds(0, width)]
        pltpu.make_async_copy(other_half, other_half, pair_recv.at[chunk]).wait()
        panel = gathered[chunk].T
        lower_first = product(panel[:, :width], upper_inv[0]).astype(BF16)
        second = (panel[:, width:].astype(F32) - product(lower_first, mid[...])).astype(BF16)
        lower_second = product(second, upper_inv[1]).astype(BF16)
        lower_block = jnp.concatenate([lower_first, lower_second], axis=1)
        where = pl.ds(pl.multiple_of(chunk * rows, rows), rows)
        out[where, :] = (
            out[where, :].astype(F32) - product(lower_block, factors[...])
        ).astype(BF16)

    def loop(count, body):
        lax.fori_loop(0, count, lambda i, carry: (body(i), carry)[1], 0)

    loop(BATCH, send_own)
    for step in range(1, n_row):
        pltpu.make_async_remote_copy(
            src_ref=head_full.at[head_rows],
            dst_ref=head_full.at[head_rows],
            send_sem=head_send,
            recv_sem=head_recv,
            device_id=((row + step) % n_row, col),
            device_id_type=MESH,
        ).start()
    for copy in small_copies:
        copy.wait()
    mid[...] = product(lower_inv[0], coupling[0]).astype(BF16)
    lower_head = product(coupling[1], upper_inv[0]).astype(BF16)

    def second_hop(chunk):
        forward(0, 1, chunk)
        forward(1, 1, chunk)

    def third_hop(base):
        def body(i):
            forward(0, 2, base + (2 * i) % BATCH + (2 * i) // BATCH)
            forward(1, 2, base + (2 * i + 1) % BATCH - (2 * i) // BATCH)
        return body

    loop(BATCH, second_hop)

    others = head_full.at[pl.ds(0, head_share * (n_row - 1))]
    pltpu.make_async_copy(others, others, head_recv).wait()
    upper_first = product(lower_inv[0], head_full[:width]).astype(BF16)
    head_second = (
        head_full[width:].astype(F32) - product(lower_head, upper_first)
    ).astype(BF16)
    factors[:width] = upper_first
    factors[width:] = product(lower_inv[1], head_second).astype(BF16)

    loop(BATCH, third_hop(0))

    def last_hop(base, next_base):
        def body(i):
            even, odd = base + 2 * i, base + 2 * i + 1
            if next_base is not None:
                send_own(next_base + 2 * i)
            forward(0, 3, even)
            forward(1, 3, odd)
            if next_base is not None:
                send_own(next_base + 2 * i + 1)
        return body

    def last_keep(base):
        def body(i):
            even, odd = base + 2 * i, base + 2 * i + 1
            keep(1, 3, even)
            keep(0, 3, odd)
        return body

    loop(half, last_hop(0, BATCH))
    loop(half, last_keep(0))

    def finish(base):
        def body(i):
            keep(0, 4, base + 2 * i)
            keep(1, 4, base + 2 * i + 1)
        return body

    def second_hop_late(i):
        second_hop(BATCH + i)

    loop(half, second_hop_late)
    loop(half, finish(0))

    def second_hop_compute(i):
        second_hop(BATCH + half + i)
        compute(i)

    loop(half, second_hop_compute)

    third = third_hop(BATCH)
    loop(half, third)

    def third_hop_compute(i):
        third(half + i)
        compute(half + i)

    loop(half, third_hop_compute)
    loop(half, last_hop(BATCH, None))
    loop(half, last_keep(BATCH))
    finish(BATCH)(0)

    done = finish(BATCH)

    def done_compute(i):
        done(i + 1)
        compute(BATCH + 2 * i)
        compute(BATCH + 2 * i + 1)

    loop(half - 1, done_compute)
    compute(CHUNKS - 2)
    compute(CHUNKS - 1)

    sent = gathered.at[:, pl.ds(0, share * (depth - 1))]
    pltpu.make_async_copy(sent, sent, ring_send).wait()
    shared = gathered.at[:, pl.ds(0, share * depth)]
    pltpu.make_async_copy(shared, shared, pair_send).wait()
    pltpu.make_async_copy(others, others, head_send).wait()


def write_kernel(result, out, sem):
    parts = 8
    rows = result.shape[0] // parts
    copies = [
        pltpu.make_async_copy(
            result.at[pl.ds(at * rows, rows)], out.at[pl.ds(at * rows, rows)], sem.at[at]
        )
        for at in range(parts)
    ]
    for copy in copies:
        copy.start()
    for copy in copies:
        copy.wait()


def on_device(trailing_slab, panel_cols, head_slab, coupling, lower_inverses, upper_inverses):
    height, columns = trailing_slab.shape
    width = coupling.shape[1]
    rows = height // CHUNKS
    dma = pltpu.SemaphoreType.DMA
    anywhere = pl.BlockSpec(memory_space=pltpu.HBM)
    result = pl.pallas_call(
        update_kernel,
        out_shape=jax.ShapeDtypeStruct((height, columns), BF16),
        in_specs=[anywhere] * 6,
        out_specs=pl.BlockSpec(memory_space=pltpu.VMEM),
        scratch_shapes=[
            pltpu.VMEM((CHUNKS, 2 * width, rows), BF16),
            pltpu.VMEM((2 * width, columns), BF16),
            pltpu.VMEM(coupling.shape, BF16),
            pltpu.VMEM(lower_inverses.shape, BF16),
            pltpu.VMEM(upper_inverses.shape, BF16),
            pltpu.VMEM((width, width), BF16),
            pltpu.VMEM((2 * width, columns), BF16),
            dma((6,)),
            dma(()),
            dma(()),
            dma(()),
            dma((2, 4, CHUNKS)),
            dma((CHUNKS,)),
            dma(()),
        ],
        compiler_params=pltpu.CompilerParams(
            collective_id=0, has_side_effects=True, vmem_limit_bytes=40 << 20
        ),
        name="gather_and_update",
    )(*[
        pltpu.with_memory_space_constraint(value, pltpu.HBM)
        for value in (
            trailing_slab, panel_cols.T, head_slab, coupling, lower_inverses, upper_inverses
        )
    ])
    return pl.pallas_call(
        write_kernel,
        out_shape=jax.ShapeDtypeStruct((height, columns), BF16),
        in_specs=[pl.BlockSpec(memory_space=pltpu.VMEM)],
        out_specs=anywhere,
        scratch_shapes=[dma((8,))],
        compiler_params=pltpu.CompilerParams(vmem_limit_bytes=16 << 20),
        name="write_result",
    )(result)


def solution(mesh):
    in_specs = (P("row", "col"), P("row", "col"), P("row", "col"), P(), P(), P())
    out_specs = P("row", "col")
    return jax.shard_map(
        on_device, mesh=mesh, in_specs=in_specs, out_specs=out_specs, check_vma=False
    )
```

```python
import functools

import jax
import jax.numpy as jnp
from jax import lax
from jax.experimental import pallas as pl
from jax.experimental.pallas import tpu as pltpu
from jax.sharding import PartitionSpec as P

MESH = pl.DeviceIdType.MESH
BF16 = jnp.bfloat16
F32 = jnp.float32
GROUP = 4
GROUPS = 3
CHUNKS = GROUP * GROUPS


def product(left, right):
    return jnp.dot(left, right, preferred_element_type=F32)


def updated_rows(gathered, chunk, slab_part, upper_inv, mid, factors):
    width = mid.shape[0]
    panel = jnp.concatenate([gathered[chunk].T, gathered[chunk + 1].T], axis=0)
    lower_first = product(panel[:, :width], upper_inv[0]).astype(BF16)
    second = (panel[:, width:].astype(F32) - product(lower_first, mid[...])).astype(BF16)
    lower_second = product(second, upper_inv[1]).astype(BF16)
    lower_block = jnp.concatenate([lower_first, lower_second], axis=1)
    return (slab_part.astype(F32) - product(lower_block, factors[...])).astype(BF16)


def update_kernel(
    slab_hbm, panel_hbm, head_hbm, coupling_hbm, lower_hbm, upper_hbm,
    out, gathered, upper_inv, mid, factors,
    head_full, coupling, lower_inv,
    local_sem, ring_send, pair_send, head_send, ring_recv, pair_recv, head_recv,
):
    chunks, width2, rows = gathered.shape
    width = width2 // 2
    share = panel_hbm.shape[0]
    head_share = head_hbm.shape[0]
    row = lax.axis_index("row")
    col = lax.axis_index("col")
    n_row = lax.axis_size("row")
    depth = lax.axis_size("col") // 2
    z, core = col // 2, col % 2
    ahead = ((z + 1) % depth) * 2 + core
    behind = ((z + depth - 1) % depth) * 2 + core
    other = z * 2 + (1 - core)

    barrier = pltpu.get_barrier_semaphore()
    for peer in (ahead, behind, other):
        pl.semaphore_signal(barrier, inc=1, device_id=(row, peer), device_id_type=MESH)
    for step in range(1, n_row):
        pl.semaphore_signal(
            barrier, inc=1, device_id=((row + step) % n_row, col), device_id_type=MESH
        )

    def block_rows(hops):
        source = ((z + depth - hops) % depth) * 2 + core
        return pl.ds(pl.multiple_of(source * share, share), share)

    own_rows = block_rows(0)
    head_rows = pl.ds(pl.multiple_of(row * head_share, head_share), head_share)

    for chunk in range(chunks):
        pltpu.make_async_copy(
            panel_hbm.at[:, pl.ds(chunk * rows, rows)],
            gathered.at[chunk, own_rows],
            local_sem.at[0],
        ).start()
    head_copy = pltpu.make_async_copy(head_hbm, head_full.at[head_rows], local_sem.at[1])
    head_copy.start()
    small_copies = [
        pltpu.make_async_copy(source, target, local_sem.at[at])
        for source, target, at in (
            (coupling_hbm, coupling, 2), (lower_hbm, lower_inv, 3), (upper_hbm, upper_inv, 4),
            (slab_hbm, out, 5),
        )
    ]
    for copy in small_copies:
        copy.start()
    pltpu.make_async_copy(
        gathered.at[:, own_rows], gathered.at[:, own_rows], local_sem.at[0]
    ).wait()
    head_copy.wait()
    pl.semaphore_wait(barrier, 3 + n_row - 1)

    def ring_copy(direction, hop, chunk):
        hops = hop - 1 if direction == 0 else depth - (hop - 1)
        where = block_rows(hops)
        return pltpu.make_async_remote_copy(
            src_ref=gathered.at[chunk, where],
            dst_ref=gathered.at[chunk, where],
            send_sem=ring_send,
            recv_sem=ring_recv.at[direction, hop - 1, chunk],
            device_id=(row, ahead if direction == 0 else behind),
            device_id_type=MESH,
        )

    def ring_arrived(direction, hop, chunk):
        hops = hop if direction == 0 else depth - hop
        where = block_rows(hops)
        pltpu.make_async_remote_copy(
            src_ref=gathered.at[chunk, where],
            dst_ref=gathered.at[chunk, where],
            send_sem=ring_send,
            recv_sem=ring_recv.at[direction, hop - 1, chunk],
            device_id=(row, ahead if direction == 0 else behind),
            device_id_type=MESH,
        ).wait_recv()

    def pair_copy(direction, hop, chunk):
        hops = hop if direction == 0 else depth - hop
        where = block_rows(hops)
        return pltpu.make_async_remote_copy(
            src_ref=gathered.at[chunk, where],
            dst_ref=gathered.at[chunk, where],
            send_sem=pair_send,
            recv_sem=pair_recv.at[chunk],
            device_id=(row, other),
            device_id_type=MESH,
        )

    def send_own(chunk):
        ring_copy(0, 1, chunk).start()
        ring_copy(1, 1, chunk).start()
        pair_copy(0, 0, chunk).start()

    def forward(direction, hop, chunk):
        ring_arrived(direction, hop, chunk)
        ring_copy(direction, hop + 1, chunk).start()
        pair_copy(direction, hop, chunk).start()

    def keep(direction, hop, chunk):
        ring_arrived(direction, hop, chunk)
        pair_copy(direction, hop, chunk).start()

    def pair_arrived(chunk):
        other_half = gathered.at[chunk, pl.ds(0, width)]
        pltpu.make_async_copy(other_half, other_half, pair_recv.at[chunk]).wait()

    def update(group, i):
        chunk = group * GROUP + 2 * i
        pair_arrived(chunk)
        pair_arrived(chunk + 1)
        where = pl.ds(pl.multiple_of(chunk * rows, rows), 2 * rows)
        out[where, :] = updated_rows(gathered, chunk, out[where, :], upper_inv, mid, factors)

    def loop(count, body):
        lax.fori_loop(0, count, lambda i, carry: (body(i), carry)[1], 0)

    def second(group, i):
        forward(0, 1, group * GROUP + i)
        forward(1, 1, group * GROUP + i)

    def third(group, i):
        base = group * GROUP
        turn = (2 * i) // GROUP
        forward(0, 2, base + (2 * i) % GROUP + turn)
        forward(1, 2, base + (2 * i + 1) % GROUP - turn)

    def fourth(group, i):
        forward(0, 3, group * GROUP + 2 * i)
        forward(1, 3, group * GROUP + 2 * i + 1)

    def keep_third(group, i):
        keep(1, 3, group * GROUP + 2 * i)
        keep(0, 3, group * GROUP + 2 * i + 1)

    def keep_fourth(group, i):
        keep(0, 4, group * GROUP + 2 * i)
        keep(1, 4, group * GROUP + 2 * i + 1)

    def finish(group, i):
        keep_third(group, i)
        keep_fourth(group, i)

    def run(count, *bodies):
        def body(i):
            for step, group in bodies:
                step(group, i)
        loop(count, body)

    half = GROUP // 2

    loop(2 * GROUP, send_own)
    for step in range(1, n_row):
        pltpu.make_async_remote_copy(
            src_ref=head_full.at[head_rows],
            dst_ref=head_full.at[head_rows],
            send_sem=head_send,
            recv_sem=head_recv,
            device_id=((row + step) % n_row, col),
            device_id_type=MESH,
        ).start()
    for copy in small_copies:
        copy.wait()
    mid[...] = product(lower_inv[0], coupling[0]).astype(BF16)
    lower_head = product(coupling[1], upper_inv[0]).astype(BF16)

    run(GROUP, (second, 0), (lambda group, i: send_own(group * GROUP + i), 2))
    run(GROUP, (third, 0), (second, 1))

    others = head_full.at[pl.ds(0, head_share * (n_row - 1))]
    pltpu.make_async_copy(others, others, head_recv).wait()
    upper_first = product(lower_inv[0], head_full[:width]).astype(BF16)
    head_second = (
        head_full[width:].astype(F32) - product(lower_head, upper_first)
    ).astype(BF16)
    factors[:width] = upper_first
    factors[width:] = product(lower_inv[1], head_second).astype(BF16)

    run(half, (fourth, 0))
    run(half, (third, 1), (second, 2))
    run(half, (finish, 0))
    run(half, (lambda group, i: third(group, half + i), 1), (lambda group, i: second(group, half + i), 2))
    run(half, (fourth, 1))
    update(0, 0)
    run(GROUP, (third, 2))
    update(0, 1)
    run(half, (fourth, 2))
    run(half, (finish, 1))
    update(1, 0)
    run(half, (keep_third, 2))
    update(1, 1)
    run(half, (keep_fourth, 2))
    loop(GROUP, lambda i: pair_arrived(2 * GROUP + i))

    sent = gathered.at[:, pl.ds(0, share * (depth - 1))]
    pltpu.make_async_copy(sent, sent, ring_send).wait()
    shared = gathered.at[:, pl.ds(0, share * depth)]
    pltpu.make_async_copy(shared, shared, pair_send).wait()
    pltpu.make_async_copy(others, others, head_send).wait()


def last_kernel(result, gathered, upper_inv, mid, factors, out, last, sem):
    rows = 2 * gathered.shape[2]
    blocks = result.shape[0] // rows
    ready = blocks - last.shape[0]

    def copy(at):
        source = result.at[pl.ds(at * rows, rows)] if at < ready else last.at[at - ready]
        return pltpu.make_async_copy(source, out.at[pl.ds(at * rows, rows)], sem.at[at])

    for at in range(ready):
        copy(at).start()
    for at in range(ready, blocks):
        last[at - ready] = updated_rows(
            gathered, 2 * at, result[pl.ds(at * rows, rows), :], upper_inv, mid, factors
        )
        copy(at).start()
    for at in range(blocks):
        copy(at).wait()


def on_device(trailing_slab, panel_cols, head_slab, coupling, lower_inverses, upper_inverses):
    height, columns = trailing_slab.shape
    width = coupling.shape[1]
    rows = height // CHUNKS
    dma = pltpu.SemaphoreType.DMA
    anywhere = pl.BlockSpec(memory_space=pltpu.HBM)
    shape = jax.ShapeDtypeStruct
    on_chip = pl.BlockSpec(memory_space=pltpu.VMEM)
    kept = pl.pallas_call(
        update_kernel,
        out_shape=[
            shape((height, columns), BF16),
            shape((CHUNKS, 2 * width, rows), BF16),
            shape(upper_inverses.shape, BF16),
            shape((width, width), BF16),
            shape((2 * width, columns), BF16),
        ],
        in_specs=[anywhere] * 6,
        out_specs=[on_chip] * 5,
        scratch_shapes=[
            pltpu.VMEM((2 * width, columns), BF16),
            pltpu.VMEM(coupling.shape, BF16),
            pltpu.VMEM(lower_inverses.shape, BF16),
            dma((6,)),
            dma(()),
            dma(()),
            dma(()),
            dma((2, 4, CHUNKS)),
            dma((CHUNKS,)),
            dma(()),
        ],
        compiler_params=pltpu.CompilerParams(
            collective_id=0, has_side_effects=True, vmem_limit_bytes=40 << 20
        ),
        name="gather_and_update",
    )(*[
        pltpu.with_memory_space_constraint(value, pltpu.HBM)
        for value in (
            trailing_slab, panel_cols.T, head_slab, coupling, lower_inverses, upper_inverses
        )
    ])
    return pl.pallas_call(
        last_kernel,
        out_shape=shape((height, columns), BF16),
        in_specs=[on_chip] * 5,
        out_specs=anywhere,
        scratch_shapes=[
            pltpu.VMEM((GROUP // 2, 2 * rows, columns), BF16),
            dma((CHUNKS // 2,)),
        ],
        compiler_params=pltpu.CompilerParams(vmem_limit_bytes=24 << 20),
        name="update_last_and_write",
    )(*kept)


def solution(mesh):
    in_specs = (P("row", "col"), P("row", "col"), P("row", "col"), P(), P(), P())
    out_specs = P("row", "col")
    return jax.shard_map(
        on_device, mesh=mesh, in_specs=in_specs, out_specs=out_specs, check_vma=False
    )
```

```python
import functools

import jax
import jax.numpy as jnp
from jax import lax
from jax.experimental import pallas as pl
from jax.experimental.pallas import tpu as pltpu
from jax.sharding import PartitionSpec as P

MESH = pl.DeviceIdType.MESH
BF16 = jnp.bfloat16
F32 = jnp.float32
GROUP = 4
GROUPS = 3
CHUNKS = GROUP * GROUPS


def product(left, right):
    return jnp.dot(left, right, preferred_element_type=F32)


def updated_rows(gathered, chunk, slab_part, upper_inv, mid, factors):
    width = mid.shape[0]
    panel = jnp.concatenate([gathered[chunk].T, gathered[chunk + 1].T], axis=0)
    lower_first = product(panel[:, :width], upper_inv[0]).astype(BF16)
    second = (panel[:, width:].astype(F32) - product(lower_first, mid[...])).astype(BF16)
    lower_second = product(second, upper_inv[1]).astype(BF16)
    lower_block = jnp.concatenate([lower_first, lower_second], axis=1)
    return (slab_part.astype(F32) - product(lower_block, factors[...])).astype(BF16)


def update_kernel(
    slab_hbm, panel_hbm, head_hbm, coupling_hbm, lower_hbm, upper_hbm,
    out, gathered, upper_inv, mid, factors,
    head_full, coupling, lower_inv,
    own_sem, local_sem, ring_send, pair_send, head_send, ring_recv, pair_recv, head_recv,
):
    chunks, width2, rows = gathered.shape
    width = width2 // 2
    share = panel_hbm.shape[0]
    head_share = head_hbm.shape[0]
    row = lax.axis_index("row")
    col = lax.axis_index("col")
    n_row = lax.axis_size("row")
    depth = lax.axis_size("col") // 2
    z, core = col // 2, col % 2
    ahead = ((z + 1) % depth) * 2 + core
    behind = ((z + depth - 1) % depth) * 2 + core
    other = z * 2 + (1 - core)

    barrier = pltpu.get_barrier_semaphore()
    for peer in (ahead, behind, other):
        pl.semaphore_signal(barrier, inc=1, device_id=(row, peer), device_id_type=MESH)

    def block_rows(hops):
        source = ((z + depth - hops) % depth) * 2 + core
        return pl.ds(pl.multiple_of(source * share, share), share)

    own_rows = block_rows(0)
    head_rows = pl.ds(pl.multiple_of(row * head_share, head_share), head_share)

    def own_copy(chunk):
        return pltpu.make_async_copy(
            panel_hbm.at[:, pl.ds(pl.multiple_of(chunk * rows, rows), rows)],
            gathered.at[chunk, own_rows],
            own_sem.at[chunk],
        )

    for chunk in range(chunks):
        own_copy(chunk).start()
    for step in range(1, n_row):
        pl.semaphore_signal(
            barrier, inc=1, device_id=((row + step) % n_row, col), device_id_type=MESH
        )

    head_copy = pltpu.make_async_copy(head_hbm, head_full.at[head_rows], local_sem.at[0])
    head_copy.start()
    small_copies = [
        pltpu.make_async_copy(source, target, local_sem.at[at])
        for source, target, at in (
            (coupling_hbm, coupling, 1), (lower_hbm, lower_inv, 2), (upper_hbm, upper_inv, 3),
            (slab_hbm, out, 4),
        )
    ]
    pl.semaphore_wait(barrier, 3 + n_row - 1)

    def ring_copy(direction, hop, chunk):
        hops = hop - 1 if direction == 0 else depth - (hop - 1)
        where = block_rows(hops)
        return pltpu.make_async_remote_copy(
            src_ref=gathered.at[chunk, where],
            dst_ref=gathered.at[chunk, where],
            send_sem=ring_send,
            recv_sem=ring_recv.at[direction, hop - 1, chunk],
            device_id=(row, ahead if direction == 0 else behind),
            device_id_type=MESH,
        )

    def ring_arrived(direction, hop, chunk):
        hops = hop if direction == 0 else depth - hop
        where = block_rows(hops)
        pltpu.make_async_remote_copy(
            src_ref=gathered.at[chunk, where],
            dst_ref=gathered.at[chunk, where],
            send_sem=ring_send,
            recv_sem=ring_recv.at[direction, hop - 1, chunk],
            device_id=(row, ahead if direction == 0 else behind),
            device_id_type=MESH,
        ).wait_recv()

    def pair_copy(direction, hop, chunk):
        hops = hop if direction == 0 else depth - hop
        where = block_rows(hops)
        return pltpu.make_async_remote_copy(
            src_ref=gathered.at[chunk, where],
            dst_ref=gathered.at[chunk, where],
            send_sem=pair_send,
            recv_sem=pair_recv.at[chunk],
            device_id=(row, other),
            device_id_type=MESH,
        )

    def send_own(chunk):
        own_copy(chunk).wait()
        ring_copy(0, 1, chunk).start()
        ring_copy(1, 1, chunk).start()
        pair_copy(0, 0, chunk).start()

    def forward(hop, chunk_up, chunk_down):
        ring_arrived(0, hop, chunk_up)
        ring_copy(0, hop + 1, chunk_up).start()
        ring_arrived(1, hop, chunk_down)
        ring_copy(1, hop + 1, chunk_down).start()
        pair_copy(0, hop, chunk_up).start()
        pair_copy(1, hop, chunk_down).start()

    def keep(direction, hop, chunk):
        ring_arrived(direction, hop, chunk)
        pair_copy(direction, hop, chunk).start()

    def pair_arrived(chunk):
        other_half = gathered.at[chunk, pl.ds(0, width)]
        pltpu.make_async_copy(other_half, other_half, pair_recv.at[chunk]).wait()

    def update(group, i):
        chunk = group * GROUP + 2 * i
        pair_arrived(chunk)
        pair_arrived(chunk + 1)
        where = pl.ds(pl.multiple_of(chunk * rows, rows), 2 * rows)
        out[where, :] = updated_rows(gathered, chunk, out[where, :], upper_inv, mid, factors)

    def loop(count, body):
        lax.fori_loop(0, count, lambda i, carry: (body(i), carry)[1], 0)

    def second(group, i):
        forward(1, group * GROUP + i, group * GROUP + i)

    def third(group, i):
        base = group * GROUP
        turn = (2 * i) // GROUP
        forward(2, base + (2 * i) % GROUP + turn, base + (2 * i + 1) % GROUP - turn)

    def fourth(group, i):
        forward(3, group * GROUP + 2 * i, group * GROUP + 2 * i + 1)

    def keep_third(group, i):
        keep(1, 3, group * GROUP + 2 * i)
        keep(0, 3, group * GROUP + 2 * i + 1)

    def keep_fourth(group, i):
        keep(0, 4, group * GROUP + 2 * i)
        keep(1, 4, group * GROUP + 2 * i + 1)

    def finish(group, i):
        keep_third(group, i)
        keep_fourth(group, i)

    def run(count, *bodies):
        def body(i):
            for step, group in bodies:
                step(group, i)
        loop(count, body)

    half = GROUP // 2

    loop(2 * GROUP, send_own)
    for copy in small_copies:
        copy.start()
    head_copy.wait()
    for step in range(1, n_row):
        pltpu.make_async_remote_copy(
            src_ref=head_full.at[head_rows],
            dst_ref=head_full.at[head_rows],
            send_sem=head_send,
            recv_sem=head_recv,
            device_id=((row + step) % n_row, col),
            device_id_type=MESH,
        ).start()
    for copy in small_copies:
        copy.wait()
    mid[...] = product(lower_inv[0], coupling[0]).astype(BF16)
    lower_head = product(coupling[1], upper_inv[0]).astype(BF16)

    run(GROUP, (second, 0), (lambda group, i: send_own(group * GROUP + i), 2))
    run(GROUP, (third, 0), (second, 1))

    others = head_full.at[pl.ds(0, head_share * (n_row - 1))]
    pltpu.make_async_copy(others, others, head_recv).wait()
    upper_first = product(lower_inv[0], head_full[:width]).astype(BF16)
    head_second = (
        head_full[width:].astype(F32) - product(lower_head, upper_first)
    ).astype(BF16)
    factors[:width] = upper_first
    factors[width:] = product(lower_inv[1], head_second).astype(BF16)

    run(half, (fourth, 0))
    run(half, (third, 1), (second, 2))
    run(half, (finish, 0))
    run(half, (lambda group, i: third(group, half + i), 1), (lambda group, i: second(group, half + i), 2))
    run(half, (third, 2))
    fourth(1, 0)
    update(0, 0)
    third(2, 2)
    fourth(1, 1)
    third(2, 3)
    update(0, 1)
    run(half, (fourth, 2))
    run(half, (finish, 1))
    run(half, (keep_third, 2))
    update(1, 0)
    run(half, (keep_fourth, 2))
    update(1, 1)
    loop(GROUP, lambda i: pair_arrived(2 * GROUP + i))

    sent = gathered.at[:, pl.ds(0, share * (depth - 1))]
    pltpu.make_async_copy(sent, sent, ring_send).wait()
    shared = gathered.at[:, pl.ds(0, share * depth)]
    pltpu.make_async_copy(shared, shared, pair_send).wait()
    pltpu.make_async_copy(others, others, head_send).wait()


def last_kernel(result, gathered, upper_inv, mid, factors, out, last, sem):
    rows = 2 * gathered.shape[2]
    blocks = result.shape[0] // rows
    ready = blocks - last.shape[0]

    def copy(at):
        source = result.at[pl.ds(at * rows, rows)] if at < ready else last.at[at - ready]
        return pltpu.make_async_copy(source, out.at[pl.ds(at * rows, rows)], sem.at[at])

    for at in range(ready):
        copy(at).start()
    for at in range(ready, blocks):
        last[at - ready] = updated_rows(
            gathered, 2 * at, result[pl.ds(at * rows, rows), :], upper_inv, mid, factors
        )
        copy(at).start()
    for at in range(blocks):
        copy(at).wait()


def on_device(trailing_slab, panel_cols, head_slab, coupling, lower_inverses, upper_inverses):
    height, columns = trailing_slab.shape
    width = coupling.shape[1]
    rows = height // CHUNKS
    dma = pltpu.SemaphoreType.DMA
    anywhere = pl.BlockSpec(memory_space=pltpu.HBM)
    shape = jax.ShapeDtypeStruct
    on_chip = pl.BlockSpec(memory_space=pltpu.VMEM)
    kept = pl.pallas_call(
        update_kernel,
        out_shape=[
            shape((height, columns), BF16),
            shape((CHUNKS, 2 * width, rows), BF16),
            shape(upper_inverses.shape, BF16),
            shape((width, width), BF16),
            shape((2 * width, columns), BF16),
        ],
        in_specs=[anywhere] * 6,
        out_specs=[on_chip] * 5,
        scratch_shapes=[
            pltpu.VMEM((2 * width, columns), BF16),
            pltpu.VMEM(coupling.shape, BF16),
            pltpu.VMEM(lower_inverses.shape, BF16),
            dma((CHUNKS,)),
            dma((5,)),
            dma(()),
            dma(()),
            dma(()),
            dma((2, 4, CHUNKS)),
            dma((CHUNKS,)),
            dma(()),
        ],
        compiler_params=pltpu.CompilerParams(
            collective_id=0, has_side_effects=True, vmem_limit_bytes=40 << 20
        ),
        name="gather_and_update",
    )(*[
        pltpu.with_memory_space_constraint(value, pltpu.HBM)
        for value in (
            trailing_slab, panel_cols.T, head_slab, coupling, lower_inverses, upper_inverses
        )
    ])
    return pl.pallas_call(
        last_kernel,
        out_shape=shape((height, columns), BF16),
        in_specs=[on_chip] * 5,
        out_specs=anywhere,
        scratch_shapes=[
            pltpu.VMEM((GROUP // 2, 2 * rows, columns), BF16),
            dma((CHUNKS // 2,)),
        ],
        compiler_params=pltpu.CompilerParams(vmem_limit_bytes=24 << 20),
        name="update_last_and_write",
    )(*kept)


def solution(mesh):
    in_specs = (P("row", "col"), P("row", "col"), P("row", "col"), P(), P(), P())
    out_specs = P("row", "col")
    return jax.shard_map(
        on_device, mesh=mesh, in_specs=in_specs, out_specs=out_specs, check_vma=False
    )
```

```python
import functools

import jax
import jax.numpy as jnp
from jax import lax
from jax.experimental import pallas as pl
from jax.experimental.pallas import tpu as pltpu
from jax.sharding import PartitionSpec as P

MESH = pl.DeviceIdType.MESH
BF16 = jnp.bfloat16
F32 = jnp.float32
GROUP = 4
GROUPS = 3
CHUNKS = GROUP * GROUPS


def product(left, right):
    return jnp.dot(left, right, preferred_element_type=F32)


def updated_rows(gathered, chunk, slab_part, upper_inv, mid, factors):
    width = mid.shape[0]
    panel = jnp.concatenate([gathered[chunk].T, gathered[chunk + 1].T], axis=0)
    lower_first = product(panel[:, :width], upper_inv[0]).astype(BF16)
    second = (panel[:, width:].astype(F32) - product(lower_first, mid[...])).astype(BF16)
    lower_second = product(second, upper_inv[1]).astype(BF16)
    lower_block = jnp.concatenate([lower_first, lower_second], axis=1)
    return (slab_part.astype(F32) - product(lower_block, factors[...])).astype(BF16)


def update_kernel(
    slab_hbm, panel_hbm, head_hbm, coupling_hbm, lower_hbm, upper_hbm,
    out, gathered, upper_inv, mid, factors,
    head_full, coupling, lower_inv,
    own_sem, local_sem, ring_send, pair_send, head_send, ring_recv, pair_recv, head_recv,
):
    chunks, width2, rows = gathered.shape
    width = width2 // 2
    share = panel_hbm.shape[0]
    head_share = head_hbm.shape[0]
    row = lax.axis_index("row")
    col = lax.axis_index("col")
    n_row = lax.axis_size("row")
    depth = lax.axis_size("col") // 2
    z, core = col // 2, col % 2
    ahead = ((z + 1) % depth) * 2 + core
    behind = ((z + depth - 1) % depth) * 2 + core
    other = z * 2 + (1 - core)

    barrier = pltpu.get_barrier_semaphore()
    for peer in (ahead, behind, other):
        pl.semaphore_signal(barrier, inc=1, device_id=(row, peer), device_id_type=MESH)

    def block_rows(hops):
        source = ((z + depth - hops) % depth) * 2 + core
        return pl.ds(pl.multiple_of(source * share, share), share)

    own_rows = block_rows(0)
    head_rows = pl.ds(pl.multiple_of(row * head_share, head_share), head_share)

    def own_copy(chunk):
        return pltpu.make_async_copy(
            panel_hbm.at[:, pl.ds(pl.multiple_of(chunk * rows, rows), rows)],
            gathered.at[chunk, own_rows],
            own_sem.at[chunk],
        )

    for chunk in range(chunks):
        own_copy(chunk).start()
    for step in range(1, n_row):
        pl.semaphore_signal(
            barrier, inc=1, device_id=((row + step) % n_row, col), device_id_type=MESH
        )

    head_copy = pltpu.make_async_copy(head_hbm, head_full.at[head_rows], local_sem.at[0])
    head_copy.start()
    small_copies = [
        pltpu.make_async_copy(source, target, local_sem.at[at])
        for source, target, at in (
            (coupling_hbm, coupling, 1), (lower_hbm, lower_inv, 2), (upper_hbm, upper_inv, 3),
        )
    ]
    def slab_copy(group, i):
        where = pl.ds(pl.multiple_of((group * GROUP + i) * rows, rows), rows)
        pltpu.make_async_copy(slab_hbm.at[where], out.at[where], local_sem.at[4]).start()

    pl.semaphore_wait(barrier, 3 + n_row - 1)

    def ring_copy(direction, hop, chunk):
        hops = hop - 1 if direction == 0 else depth - (hop - 1)
        where = block_rows(hops)
        return pltpu.make_async_remote_copy(
            src_ref=gathered.at[chunk, where],
            dst_ref=gathered.at[chunk, where],
            send_sem=ring_send,
            recv_sem=ring_recv.at[direction, hop - 1, chunk],
            device_id=(row, ahead if direction == 0 else behind),
            device_id_type=MESH,
        )

    def ring_arrived(direction, hop, chunk):
        hops = hop if direction == 0 else depth - hop
        where = block_rows(hops)
        pltpu.make_async_remote_copy(
            src_ref=gathered.at[chunk, where],
            dst_ref=gathered.at[chunk, where],
            send_sem=ring_send,
            recv_sem=ring_recv.at[direction, hop - 1, chunk],
            device_id=(row, ahead if direction == 0 else behind),
            device_id_type=MESH,
        ).wait_recv()

    def pair_copy(direction, hop, chunk):
        hops = hop if direction == 0 else depth - hop
        where = block_rows(hops)
        return pltpu.make_async_remote_copy(
            src_ref=gathered.at[chunk, where],
            dst_ref=gathered.at[chunk, where],
            send_sem=pair_send,
            recv_sem=pair_recv.at[chunk],
            device_id=(row, other),
            device_id_type=MESH,
        )

    def send_own(chunk):
        own_copy(chunk).wait()
        ring_copy(0, 1, chunk).start()
        ring_copy(1, 1, chunk).start()
        pair_copy(0, 0, chunk).start()

    def forward(hop, chunk_up, chunk_down):
        ring_arrived(0, hop, chunk_up)
        ring_copy(0, hop + 1, chunk_up).start()
        ring_arrived(1, hop, chunk_down)
        ring_copy(1, hop + 1, chunk_down).start()
        pair_copy(0, hop, chunk_up).start()
        pair_copy(1, hop, chunk_down).start()

    def keep(direction, hop, chunk):
        ring_arrived(direction, hop, chunk)
        pair_copy(direction, hop, chunk).start()

    def pair_arrived(chunk):
        other_half = gathered.at[chunk, pl.ds(0, width)]
        pltpu.make_async_copy(other_half, other_half, pair_recv.at[chunk]).wait()

    def update(group, i):
        chunk = group * GROUP + 2 * i
        pair_arrived(chunk)
        pair_arrived(chunk + 1)
        where = pl.ds(pl.multiple_of(chunk * rows, rows), 2 * rows)
        out[where, :] = updated_rows(gathered, chunk, out[where, :], upper_inv, mid, factors)

    def loop(count, body):
        lax.fori_loop(0, count, lambda i, carry: (body(i), carry)[1], 0)

    def second(group, i):
        forward(1, group * GROUP + i, group * GROUP + i)

    def third(group, i):
        base = group * GROUP
        turn = (2 * i) // GROUP
        forward(2, base + (2 * i) % GROUP + turn, base + (2 * i + 1) % GROUP - turn)

    def fourth(group, i):
        forward(3, group * GROUP + 2 * i, group * GROUP + 2 * i + 1)

    def keep_third(group, i):
        keep(1, 3, group * GROUP + 2 * i)
        keep(0, 3, group * GROUP + 2 * i + 1)

    def keep_fourth(group, i):
        keep(0, 4, group * GROUP + 2 * i)
        keep(1, 4, group * GROUP + 2 * i + 1)

    def finish(group, i):
        keep_third(group, i)
        keep_fourth(group, i)

    def run(count, *bodies):
        def body(i):
            for step, group in bodies:
                step(group, i)
        loop(count, body)

    half = GROUP // 2

    loop(2 * GROUP, send_own)
    for copy in small_copies:
        copy.start()
    head_copy.wait()
    for step in range(1, n_row):
        pltpu.make_async_remote_copy(
            src_ref=head_full.at[head_rows],
            dst_ref=head_full.at[head_rows],
            send_sem=head_send,
            recv_sem=head_recv,
            device_id=((row + step) % n_row, col),
            device_id_type=MESH,
        ).start()
    for copy in small_copies:
        copy.wait()
    mid[...] = product(lower_inv[0], coupling[0]).astype(BF16)
    lower_head = product(coupling[1], upper_inv[0]).astype(BF16)

    run(GROUP, (second, 0), (lambda group, i: send_own(group * GROUP + i), 2), (slab_copy, 0))
    run(GROUP, (third, 0), (second, 1), (slab_copy, 1))

    others = head_full.at[pl.ds(0, head_share * (n_row - 1))]
    pltpu.make_async_copy(others, others, head_recv).wait()
    upper_first = product(lower_inv[0], head_full[:width]).astype(BF16)
    head_second = (
        head_full[width:].astype(F32) - product(lower_head, upper_first)
    ).astype(BF16)
    factors[:width] = upper_first
    factors[width:] = product(lower_inv[1], head_second).astype(BF16)

    run(half, (fourth, 0))
    run(half, (third, 1), (second, 2), (slab_copy, 2), (lambda group, i: slab_copy(group, half + i), 2))
    run(half, (finish, 0))
    run(half, (lambda group, i: third(group, half + i), 1), (lambda group, i: second(group, half + i), 2))
    run(half, (third, 2))
    fourth(1, 0)
    pltpu.make_async_copy(slab_hbm, out, local_sem.at[4]).wait()
    update(0, 0)
    third(2, 2)
    fourth(1, 1)
    third(2, 3)
    update(0, 1)
    run(half, (fourth, 2))
    run(half, (finish, 1))
    run(half, (keep_third, 2))
    update(1, 0)
    run(half, (keep_fourth, 2))
    update(1, 1)
    loop(GROUP, lambda i: pair_arrived(2 * GROUP + i))

    sent = gathered.at[:, pl.ds(0, share * (depth - 1))]
    pltpu.make_async_copy(sent, sent, ring_send).wait()
    shared = gathered.at[:, pl.ds(0, share * depth)]
    pltpu.make_async_copy(shared, shared, pair_send).wait()
    pltpu.make_async_copy(others, others, head_send).wait()


def last_kernel(result, gathered, upper_inv, mid, factors, out, last, sem):
    rows = 2 * gathered.shape[2]
    blocks = result.shape[0] // rows
    ready = blocks - last.shape[0]

    def copy(at):
        source = result.at[pl.ds(at * rows, rows)] if at < ready else last.at[at - ready]
        return pltpu.make_async_copy(source, out.at[pl.ds(at * rows, rows)], sem.at[at])

    for at in range(ready):
        copy(at).start()
    for at in range(ready, blocks):
        last[at - ready] = updated_rows(
            gathered, 2 * at, result[pl.ds(at * rows, rows), :], upper_inv, mid, factors
        )
        copy(at).start()
    for at in range(blocks):
        copy(at).wait()


def on_device(trailing_slab, panel_cols, head_slab, coupling, lower_inverses, upper_inverses):
    height, columns = trailing_slab.shape
    width = coupling.shape[1]
    rows = height // CHUNKS
    dma = pltpu.SemaphoreType.DMA
    anywhere = pl.BlockSpec(memory_space=pltpu.HBM)
    shape = jax.ShapeDtypeStruct
    on_chip = pl.BlockSpec(memory_space=pltpu.VMEM)
    kept = pl.pallas_call(
        update_kernel,
        out_shape=[
            shape((height, columns), BF16),
            shape((CHUNKS, 2 * width, rows), BF16),
            shape(upper_inverses.shape, BF16),
            shape((width, width), BF16),
            shape((2 * width, columns), BF16),
        ],
        in_specs=[anywhere] * 6,
        out_specs=[on_chip] * 5,
        scratch_shapes=[
            pltpu.VMEM((2 * width, columns), BF16),
            pltpu.VMEM(coupling.shape, BF16),
            pltpu.VMEM(lower_inverses.shape, BF16),
            dma((CHUNKS,)),
            dma((5,)),
            dma(()),
            dma(()),
            dma(()),
            dma((2, 4, CHUNKS)),
            dma((CHUNKS,)),
            dma(()),
        ],
        compiler_params=pltpu.CompilerParams(
            collective_id=0, has_side_effects=True, vmem_limit_bytes=40 << 20
        ),
        name="gather_and_update",
    )(*[
        pltpu.with_memory_space_constraint(value, pltpu.HBM)
        for value in (
            trailing_slab, panel_cols.T, head_slab, coupling, lower_inverses, upper_inverses
        )
    ])
    return pl.pallas_call(
        last_kernel,
        out_shape=shape((height, columns), BF16),
        in_specs=[on_chip] * 5,
        out_specs=anywhere,
        scratch_shapes=[
            pltpu.VMEM((GROUP // 2, 2 * rows, columns), BF16),
            dma((CHUNKS // 2,)),
        ],
        compiler_params=pltpu.CompilerParams(vmem_limit_bytes=24 << 20),
        name="update_last_and_write",
    )(*kept)


def solution(mesh):
    in_specs = (P("row", "col"), P("row", "col"), P("row", "col"), P(), P(), P())
    out_specs = P("row", "col")
    return jax.shard_map(
        on_device, mesh=mesh, in_specs=in_specs, out_specs=out_specs, check_vma=False
    )
```

```python
import functools

import jax
import jax.numpy as jnp
from jax import lax
from jax.experimental import pallas as pl
from jax.experimental.pallas import tpu as pltpu
from jax.sharding import PartitionSpec as P

MESH = pl.DeviceIdType.MESH
BF16 = jnp.bfloat16
F32 = jnp.float32
GROUP = 2
GROUPS = 3
CHUNKS = GROUP * GROUPS


def product(left, right):
    return jnp.dot(left, right, preferred_element_type=F32)


def updated_rows(gathered, chunk, slab_part, upper_inv, mid, factors):
    width = mid.shape[0]
    panel = gathered[chunk].T
    lower_first = product(panel[:, :width], upper_inv[0]).astype(BF16)
    second = (panel[:, width:].astype(F32) - product(lower_first, mid[...])).astype(BF16)
    lower_second = product(second, upper_inv[1]).astype(BF16)
    lower_block = jnp.concatenate([lower_first, lower_second], axis=1)
    return (slab_part.astype(F32) - product(lower_block, factors[...])).astype(BF16)


def update_kernel(
    slab_hbm, panel_hbm, head_hbm, coupling_hbm, lower_hbm, upper_hbm,
    out, gathered, upper_inv, mid, factors,
    head_full, coupling, lower_inv,
    own_sem, local_sem, ring_send, pair_send, head_send, ring_recv, pair_recv, head_recv,
):
    chunks, width2, rows = gathered.shape
    width = width2 // 2
    share = panel_hbm.shape[0]
    head_share = head_hbm.shape[0]
    row = lax.axis_index("row")
    col = lax.axis_index("col")
    n_row = lax.axis_size("row")
    depth = lax.axis_size("col") // 2
    z, core = col // 2, col % 2
    ahead = ((z + 1) % depth) * 2 + core
    behind = ((z + depth - 1) % depth) * 2 + core
    other = z * 2 + (1 - core)

    barrier = pltpu.get_barrier_semaphore()
    for peer in (ahead, behind, other):
        pl.semaphore_signal(barrier, inc=1, device_id=(row, peer), device_id_type=MESH)

    def block_rows(hops):
        source = ((z + depth - hops) % depth) * 2 + core
        return pl.ds(pl.multiple_of(source * share, share), share)

    own_rows = block_rows(0)
    head_rows = pl.ds(pl.multiple_of(row * head_share, head_share), head_share)

    def own_copy(chunk):
        return pltpu.make_async_copy(
            panel_hbm.at[:, pl.ds(pl.multiple_of(chunk * rows, rows), rows)],
            gathered.at[chunk, own_rows],
            own_sem.at[chunk],
        )

    for chunk in range(chunks):
        own_copy(chunk).start()
    for step in range(1, n_row):
        pl.semaphore_signal(
            barrier, inc=1, device_id=((row + step) % n_row, col), device_id_type=MESH
        )

    head_copy = pltpu.make_async_copy(head_hbm, head_full.at[head_rows], local_sem.at[0])
    head_copy.start()
    small_copies = [
        pltpu.make_async_copy(source, target, local_sem.at[at])
        for source, target, at in (
            (coupling_hbm, coupling, 1), (lower_hbm, lower_inv, 2), (upper_hbm, upper_inv, 3),
            (slab_hbm, out, 4),
        )
    ]
    pl.semaphore_wait(barrier, 3 + n_row - 1)

    def ring_copy(direction, hop, chunk):
        hops = hop - 1 if direction == 0 else depth - (hop - 1)
        where = block_rows(hops)
        return pltpu.make_async_remote_copy(
            src_ref=gathered.at[chunk, where],
            dst_ref=gathered.at[chunk, where],
            send_sem=ring_send,
            recv_sem=ring_recv.at[direction, hop - 1, chunk],
            device_id=(row, ahead if direction == 0 else behind),
            device_id_type=MESH,
        )

    def ring_arrived(direction, hop, chunk):
        hops = hop if direction == 0 else depth - hop
        where = block_rows(hops)
        pltpu.make_async_remote_copy(
            src_ref=gathered.at[chunk, where],
            dst_ref=gathered.at[chunk, where],
            send_sem=ring_send,
            recv_sem=ring_recv.at[direction, hop - 1, chunk],
            device_id=(row, ahead if direction == 0 else behind),
            device_id_type=MESH,
        ).wait_recv()

    def pair_copy(direction, hop, chunk):
        hops = hop if direction == 0 else depth - hop
        where = block_rows(hops)
        return pltpu.make_async_remote_copy(
            src_ref=gathered.at[chunk, where],
            dst_ref=gathered.at[chunk, where],
            send_sem=pair_send,
            recv_sem=pair_recv.at[chunk],
            device_id=(row, other),
            device_id_type=MESH,
        )

    def send_own(chunk):
        own_copy(chunk).wait()
        ring_copy(0, 1, chunk).start()
        ring_copy(1, 1, chunk).start()
        pair_copy(0, 0, chunk).start()

    def forward(hop, chunk_up, chunk_down):
        ring_arrived(0, hop, chunk_up)
        ring_copy(0, hop + 1, chunk_up).start()
        ring_arrived(1, hop, chunk_down)
        ring_copy(1, hop + 1, chunk_down).start()
        pair_copy(0, hop, chunk_up).start()
        pair_copy(1, hop, chunk_down).start()

    def keep(direction, hop, chunk):
        ring_arrived(direction, hop, chunk)
        pair_copy(direction, hop, chunk).start()

    def pair_arrived(chunk):
        other_half = gathered.at[chunk, pl.ds(0, width)]
        pltpu.make_async_copy(other_half, other_half, pair_recv.at[chunk]).wait()

    def update(group, i):
        chunk = group * GROUP + i
        pair_arrived(chunk)
        where = pl.ds(pl.multiple_of(chunk * rows, rows), rows)
        out[where, :] = updated_rows(gathered, chunk, out[where, :], upper_inv, mid, factors)

    def loop(count, body):
        lax.fori_loop(0, count, lambda i, carry: (body(i), carry)[1], 0)

    def second(group, i):
        forward(1, group * GROUP + i, group * GROUP + i)

    def third(group, i):
        base = group * GROUP
        turn = (2 * i) // GROUP
        forward(2, base + (2 * i) % GROUP + turn, base + (2 * i + 1) % GROUP - turn)

    def fourth(group, i):
        forward(3, group * GROUP + 2 * i, group * GROUP + 2 * i + 1)

    def keep_third(group, i):
        keep(1, 3, group * GROUP + 2 * i)
        keep(0, 3, group * GROUP + 2 * i + 1)

    def keep_fourth(group, i):
        keep(0, 4, group * GROUP + 2 * i)
        keep(1, 4, group * GROUP + 2 * i + 1)

    def finish(group, i):
        keep_third(group, i)
        keep_fourth(group, i)

    def run(count, *bodies):
        def body(i):
            for step, group in bodies:
                step(group, i)
        loop(count, body)

    half = GROUP // 2

    loop(2 * GROUP, send_own)
    for copy in small_copies:
        copy.start()
    head_copy.wait()
    for step in range(1, n_row):
        pltpu.make_async_remote_copy(
            src_ref=head_full.at[head_rows],
            dst_ref=head_full.at[head_rows],
            send_sem=head_send,
            recv_sem=head_recv,
            device_id=((row + step) % n_row, col),
            device_id_type=MESH,
        ).start()
    for copy in small_copies:
        copy.wait()
    mid[...] = product(lower_inv[0], coupling[0]).astype(BF16)
    lower_head = product(coupling[1], upper_inv[0]).astype(BF16)

    run(GROUP, (second, 0), (lambda group, i: send_own(group * GROUP + i), 2))
    run(GROUP, (third, 0), (second, 1))

    others = head_full.at[pl.ds(0, head_share * (n_row - 1))]
    pltpu.make_async_copy(others, others, head_recv).wait()
    upper_first = product(lower_inv[0], head_full[:width]).astype(BF16)
    head_second = (
        head_full[width:].astype(F32) - product(lower_head, upper_first)
    ).astype(BF16)
    factors[:width] = upper_first
    factors[width:] = product(lower_inv[1], head_second).astype(BF16)

    run(half, (fourth, 0))
    run(half, (third, 1), (second, 2))
    run(half, (finish, 0))
    run(half, (lambda group, i: third(group, half + i), 1), (lambda group, i: second(group, half + i), 2))
    run(half, (third, 2))
    fourth(1, 0)
    update(0, 0)
    third(2, 1)
    update(0, 1)
    run(half, (fourth, 2))
    run(half, (finish, 1))
    run(half, (keep_third, 2))
    update(1, 0)
    run(half, (keep_fourth, 2))
    update(1, 1)
    loop(GROUP, lambda i: pair_arrived(2 * GROUP + i))

    sent = gathered.at[:, pl.ds(0, share * (depth - 1))]
    pltpu.make_async_copy(sent, sent, ring_send).wait()
    shared = gathered.at[:, pl.ds(0, share * depth)]
    pltpu.make_async_copy(shared, shared, pair_send).wait()
    pltpu.make_async_copy(others, others, head_send).wait()


def last_kernel(result, gathered, upper_inv, mid, factors, out, last, sem):
    rows = gathered.shape[2]
    blocks = result.shape[0] // rows
    ready = blocks - last.shape[0]

    def copy(at):
        source = result.at[pl.ds(at * rows, rows)] if at < ready else last.at[at - ready]
        return pltpu.make_async_copy(source, out.at[pl.ds(at * rows, rows)], sem.at[at])

    for at in range(ready):
        copy(at).start()
    for at in range(ready, blocks):
        last[at - ready] = updated_rows(
            gathered, at, result[pl.ds(at * rows, rows), :], upper_inv, mid, factors
        )
        copy(at).start()
    for at in range(blocks):
        copy(at).wait()


def on_device(trailing_slab, panel_cols, head_slab, coupling, lower_inverses, upper_inverses):
    height, columns = trailing_slab.shape
    width = coupling.shape[1]
    rows = height // CHUNKS
    dma = pltpu.SemaphoreType.DMA
    anywhere = pl.BlockSpec(memory_space=pltpu.HBM)
    shape = jax.ShapeDtypeStruct
    on_chip = pl.BlockSpec(memory_space=pltpu.VMEM)
    kept = pl.pallas_call(
        update_kernel,
        out_shape=[
            shape((height, columns), BF16),
            shape((CHUNKS, 2 * width, rows), BF16),
            shape(upper_inverses.shape, BF16),
            shape((width, width), BF16),
            shape((2 * width, columns), BF16),
        ],
        in_specs=[anywhere] * 6,
        out_specs=[on_chip] * 5,
        scratch_shapes=[
            pltpu.VMEM((2 * width, columns), BF16),
            pltpu.VMEM(coupling.shape, BF16),
            pltpu.VMEM(lower_inverses.shape, BF16),
            dma((CHUNKS,)),
            dma((5,)),
            dma(()),
            dma(()),
            dma(()),
            dma((2, 4, CHUNKS)),
            dma((CHUNKS,)),
            dma(()),
        ],
        compiler_params=pltpu.CompilerParams(
            collective_id=0, has_side_effects=True, vmem_limit_bytes=40 << 20
        ),
        name="gather_and_update",
    )(*[
        pltpu.with_memory_space_constraint(value, pltpu.HBM)
        for value in (
            trailing_slab, panel_cols.T, head_slab, coupling, lower_inverses, upper_inverses
        )
    ])
    return pl.pallas_call(
        last_kernel,
        out_shape=shape((height, columns), BF16),
        in_specs=[on_chip] * 5,
        out_specs=anywhere,
        scratch_shapes=[
            pltpu.VMEM((GROUP, rows, columns), BF16),
            dma((CHUNKS,)),
        ],
        compiler_params=pltpu.CompilerParams(vmem_limit_bytes=24 << 20),
        name="update_last_and_write",
    )(*kept)


def solution(mesh):
    in_specs = (P("row", "col"), P("row", "col"), P("row", "col"), P(), P(), P())
    out_specs = P("row", "col")
    return jax.shard_map(
        on_device, mesh=mesh, in_specs=in_specs, out_specs=out_specs, check_vma=False
    )
```
